32 devices in a mesh: node: 8 (over y, x, core), local: 4 (over z).
Axes of the slice: x: 2, y: 2, z: 4, core: 2. Of those that a mesh axis runs over, the one named last changes fastest.
Arguments:
- vit_tiles: bfloat16 [8, 4, 128, 12800], P('node', 'local'), may hold values from -6 to 6
- tile_counts: int32 [8, 1], P('node'), may hold values from 1 to 2
- block_of_piece: int32 [8, 2], P('node'), may hold values from 0 to 7, as said below
- segment_ids: int32 [8, 8, 256], P('node', None, 'local'), may hold values from 0 to 15, as said below
- text_rows: bfloat16 [8, 8, 256, 3584], P('node', None, 'local'), may hold values from -6 to 6
- cotangent: bfloat16 [8, 8, 256, 512], P('node', None, 'local'), may hold values from -6 to 6
- proj_weight: bfloat16 [12800, 3584], P('local', 'node'), may hold values from -0.0546875 to 0.0546875
- proj_bias: float32 [3584], replicated, may hold values from -3 to 3
- out_weight: bfloat16 [3584, 3584], P(None, 'local'), may hold values from -0.09375 to 0.09375
- out_bias: float32 [3584], replicated, may hold values from -3 to 3
- ln_gain: float32 [12800], replicated, may hold values from 0.25 to 1.75
- ln_bias: float32 [12800], replicated, may hold values from -2 to 2
- norm_gain: float32 [3584], replicated, may hold values from 0.25 to 1.75
- v_weight: bfloat16 [3584, 512], P(('node', 'local')), may hold values from -0.09375 to 0.09375
Outputs:
- hidden_grad: bfloat16 [8, 8, 256, 3584], P('node', None, 'local')
- value_weight_grad: float32 [3584, 512], P(('node', 'local'))
- value_bias_grad: float32 [512], replicated
- norm_gain_grad: float32 [3584], replicated
The draws below stay inside these ranges and needn't reach their ends.
Inputs may be any that keep to these rules, and one draw needn't show every extreme that they name: `block_of_piece`: within one sequence the entries are distinct. `segment_ids`: along each sequence, read block by block, the ids never fall; every sequence has exactly 16 documents.
All inputs are finite; a program needn't handle non-finite values.
Results may differ from the reference program's by a relative error of at most 0.017.
Values may be sent and summed in bfloat16 or wider, within the bound.
No kernel may reach another device: no remote copies, remote signals or barrier semaphores. Data moves between devices by JAX's collectives and lax.ppermute only.
A program may use at most 128 MiB of HBM per device.

```python
import jax
import jax.numpy as jnp
from jax import lax

VW = 12800
D = 3584
KV = 512
TILE_TOK = 256
SLOTS = 2
BLOCKS = 8
DOCS = 16
HALF = 128
PIECES = 2
IMAGES = 1
N_NODE = 8
N_LOCAL = 4


def draw_block_of_piece(key, part):
    node_keys = jax.random.split(jax.random.fold_in(key, 11), N_NODE)

    def one_node(node_key):
        return jax.random.permutation(node_key, BLOCKS)[:PIECES].astype(jnp.int32)
    return jax.vmap(one_node)(node_keys)


def draw_segment_ids(key, part):
    node_keys = jax.random.split(jax.random.fold_in(key, 23), N_NODE)
    length = BLOCKS * TILE_TOK

    def one_node(node_key):
        starts = jax.random.permutation(node_key, length - 1)[:DOCS - 1] + 1
        boundary = jnp.zeros((length,), jnp.int32).at[starts].set(1)
        return jnp.cumsum(boundary).astype(jnp.int32).reshape(BLOCKS, TILE_TOK)
    return jax.vmap(one_node)(node_keys)


def set_ends(result, stream_key, smallest, top_value):
    shape = result.shape
    place = [jax.random.randint(jax.random.fold_in(stream_key, axis), (), 0, shape[axis]) for axis in range(len(shape))]
    result = result.at[tuple(place)].set(smallest)
    longest = shape.index(max(shape))
    place[longest] = (place[longest] + 1) % shape[longest]
    return result.at[tuple(place)].set(top_value)


def block_levels(stream_key, shape, cuts, smallest, high):
    factor_of, own = 1.0, jax.random.fold_in(stream_key, 6)
    for dim, parts in cuts:
        steps = jnp.exp(jax.random.uniform(jax.random.fold_in(own, dim), (parts,), jnp.float32, smallest / len(cuts), high / len(cuts)))
        factor_of = factor_of * jnp.repeat(steps, shape[dim] // parts).reshape([-1 if axis == dim else 1 for axis in range(len(shape))])
    return factor_of


def scatter_about(stream_key, dims, scale, most, shards=(), kind=jnp.bfloat16):
    result = jax.random.normal(stream_key, dims, jnp.float32) * scale
    if len(shards) > 0:
        result = block_levels(stream_key, dims, shards, -0.22, 0.18) * result
    return jnp.clip(result, min=-most, max=most).astype(kind)


def setup_inputs(seed: int = 0) -> dict:
    streams_of = jax.random.split(jax.random.key(seed), 15)
    return {
        "vit_tiles": scatter_about(streams_of[0], (N_NODE, N_LOCAL, HALF, VW), 1.0, 6.0, ((0, 8), (1, 4))),
        "tile_counts": set_ends(jax.random.randint(streams_of[1], (N_NODE, IMAGES), 1, SLOTS + 1), jax.random.fold_in(streams_of[1], 1), 1, SLOTS).astype(jnp.int32),
        "block_of_piece": draw_block_of_piece(jax.random.fold_in(streams_of[14], 71), 0),
        "segment_ids": draw_segment_ids(jax.random.fold_in(streams_of[14], 71), 0),
        "text_rows": scatter_about(streams_of[4], (N_NODE, BLOCKS, TILE_TOK, D), 1.0, 6.0, ((0, 8), (2, 4))),
        "cotangent": scatter_about(streams_of[5], (N_NODE, BLOCKS, TILE_TOK, KV), 1.0, 6.0, ((0, 8), (2, 4))),
        "proj_weight": scatter_about(streams_of[6], (VW, D), VW ** -0.5, 0.0546875, ((0, 4), (1, 8))),
        "proj_bias": scatter_about(streams_of[7], (D,), 0.5, 3.0, (), jnp.float32),
        "out_weight": scatter_about(streams_of[8], (D, D), D ** -0.5, 0.09375, ((1, 4),)),
        "out_bias": scatter_about(streams_of[9], (D,), 0.5, 3.0, (), jnp.float32),
        "ln_gain": jnp.clip(1.0 + 0.15 * jax.random.normal(streams_of[10], (VW,), jnp.float32), 0.25, 1.75),
        "ln_bias": scatter_about(streams_of[11], (VW,), 0.4, 2.0, (), jnp.float32),
        "norm_gain": jnp.clip(1.0 + 0.15 * jax.random.normal(streams_of[12], (D,), jnp.float32), 0.25, 1.75),
        "v_weight": scatter_about(streams_of[13], (D, KV), D ** -0.5, 0.09375, ((0, 32),)),
    }


def layer_norm(vit_rows, scale_vec, shift_vec):
    values = vit_rows.astype(jnp.float32)
    average = lax.optimization_barrier(jnp.mean(values, -1, keepdims=True))
    centred = values - average
    variance = lax.optimization_barrier(jnp.mean(centred * centred, -1, keepdims=True))
    return (centred * lax.rsqrt(variance + 1e-05) * scale_vec + shift_vec).astype(jnp.bfloat16)

def reference(vit_tiles, tile_counts, block_of_piece, segment_ids, text_rows, cotangent, proj_weight, proj_bias, out_weight, out_bias, ln_gain, ln_bias, norm_gain, v_weight):
    piece_total = N_LOCAL // 2
    slice_width = VW // N_LOCAL
    half_rows = TILE_TOK // 2
    run_rows = TILE_TOK // (2 * N_LOCAL)

    def one_sequence(sequence):
        normed = layer_norm(vit_tiles[sequence].reshape(N_LOCAL * half_rows, VW), ln_gain, ln_bias)
        preact = jnp.zeros((N_LOCAL * half_rows, D), jnp.float32)
        for slice_index in range(N_LOCAL):
            lower = slice_index * slice_width
            term = jnp.dot(normed[:, lower:lower + slice_width], proj_weight[lower:lower + slice_width], preferred_element_type=jnp.float32)
            term = lax.optimization_barrier(term.astype(jnp.bfloat16))
            preact = preact + term.astype(jnp.float32)
        middle = jax.nn.gelu(preact + proj_bias, approximate=False).astype(jnp.bfloat16)
        projected = (jnp.dot(middle, out_weight, preferred_element_type=jnp.float32) + out_bias).astype(jnp.bfloat16)
        projected = projected.reshape(piece_total, 2, N_LOCAL, run_rows, D).transpose(0, 2, 1, 3, 4).reshape(piece_total, TILE_TOK, D)
        filled = jnp.arange(piece_total, dtype=jnp.int32) % SLOTS < jnp.repeat(tile_counts[sequence], SLOTS)
        chosen = (block_of_piece[sequence][None, :] == jnp.arange(BLOCKS, dtype=jnp.int32)[:, None]) & filled[None, :]
        placed = jnp.einsum('bp,ptd->btd', chosen.astype(jnp.float32), projected.astype(jnp.float32))
        is_image = lax.optimization_barrier(jnp.sum(chosen.astype(jnp.int32), 1)) > 0
        hidden = jnp.where(is_image[:, None, None], placed.astype(jnp.bfloat16), text_rows[sequence])
        doc_ids = segment_ids[sequence].reshape(-1)
        doc_sizes = lax.optimization_barrier(jnp.sum((doc_ids[:, None] == jnp.arange(DOCS, dtype=jnp.int32)[None, :]).astype(jnp.float32), 0))
        doc_weight = BLOCKS * TILE_TOK / (DOCS * doc_sizes)
        token_weight = doc_weight[doc_ids]
        value_grad = (cotangent[sequence].reshape(-1, KV).astype(jnp.float32) * token_weight[:, None]).astype(jnp.bfloat16)
        hidden_f = hidden.reshape(-1, D).astype(jnp.float32)
        inv_rms = lax.rsqrt(lax.optimization_barrier(jnp.mean(hidden_f * hidden_f, -1, keepdims=True)) + 1e-06)
        normed_input = (hidden_f * inv_rms * norm_gain).astype(jnp.bfloat16)
        grad_normed = lax.dot_general(value_grad, v_weight, (((1,), (1,)), ((), ())), preferred_element_type=jnp.float32)
        gain_part = lax.optimization_barrier(jnp.sum(grad_normed * hidden_f * inv_rms, 0))
        scaled = grad_normed * norm_gain
        grad_hidden = inv_rms * scaled - hidden_f * (inv_rms * inv_rms * inv_rms) * lax.optimization_barrier(jnp.mean(scaled * hidden_f, -1, keepdims=True))
        weight_part = lax.dot_general(normed_input, value_grad, (((0,), (0,)), ((), ())), preferred_element_type=jnp.float32)
        bias_part = lax.optimization_barrier(jnp.sum(value_grad.astype(jnp.float32), 0))
        return (grad_hidden.astype(jnp.bfloat16).reshape(BLOCKS, TILE_TOK, D), weight_part, bias_part, gain_part)
    grad_hidden, weight_parts, bias_parts, gain_parts = lax.map(one_sequence, jnp.arange(N_NODE, dtype=jnp.int32))
    return (grad_hidden, lax.optimization_barrier(jnp.sum(weight_parts, 0)) / N_NODE, lax.optimization_barrier(jnp.sum(bias_parts, 0)) / N_NODE, lax.optimization_barrier(jnp.sum(gain_parts, 0)) / N_NODE)
```

```python
import jax
import jax.numpy as jnp
from jax import lax
from jax.sharding import PartitionSpec as P

SLOTS = 2
DOCS = 16


class Ring:
    def __init__(self, axis, order, lanes):
        self.axis, self.size = axis, len(order)
        steps = range(self.size)
        self.forward = [
            (order[q] * lanes + c, order[(q + 1) % self.size] * lanes + c)
            for q in steps
            for c in range(lanes)
        ]
        self.backward = [(b, a) for a, b in self.forward]

    def up(self, x):
        return lax.ppermute(x, self.axis, self.forward)

    def down(self, x):
        return lax.ppermute(x, self.axis, self.backward)


def f32(x):
    return x.astype(jnp.float32)


def bf16(x):
    return x.astype(jnp.bfloat16)


def shift(x, axis, step):
    size = lax.axis_size(axis)
    return lax.ppermute(x, axis, [(j, (j + step) % size) for j in range(size)])


def ring_gather(x, ring):
    size = ring.size
    slots = [None] * size
    slots[0] = [x]
    ahead, behind = x, x
    for step in range(1, (size - 1) // 2 + 1):
        ahead, behind = ring.up(ahead), ring.down(behind)
        slots[size - step] = [ahead]
        slots[step] = [behind]
    if size > 1 and size % 2 == 0:
        half = x.shape[0] // 2
        slots[size // 2] = [ring.up(ahead[:half]), ring.down(behind[half:])]
    return slots


def ring_scatter(slots, ring):
    size = ring.size
    if size == 1:
        return f32(slots[0])
    half = slots[0].shape[0] // 2
    up = down = None
    if size % 2 == 0:
        up = ring.up(slots[size // 2][:half])
        down = ring.down(slots[size // 2][half:])
    partial = up is not None
    for step in range((size - 1) // 2, 0, -1):
        to_up, to_down = slots[step], slots[size - step]
        if partial:
            to_up = jnp.concatenate([bf16(f32(to_up[:half]) + f32(up)), to_up[half:]], 0)
            to_down = jnp.concatenate([to_down[:half], bf16(f32(to_down[half:]) + f32(down))], 0)
        elif up is not None:
            to_up = bf16(f32(to_up) + f32(up))
            to_down = bf16(f32(to_down) + f32(down))
        partial = False
        up, down = ring.up(to_up), ring.down(to_down)
    if partial:
        return f32(slots[0]) + jnp.concatenate([f32(up), f32(down)], 0)
    return f32(slots[0]) + f32(up) + f32(down)


def exchange(chunk_for, size, axis):
    slots = [None] * size
    middle = size // 2 if size > 1 and size % 2 == 0 else None
    if middle is not None:
        chunk = chunk_for(middle)
        half = chunk.shape[0] // 2
        first, second = shift(chunk[:half], axis, 1), shift(chunk[half:], axis, -1)
        if middle > 1:
            first, second = shift(first, axis, middle - 1), shift(second, axis, 1 - middle)
        slots[middle] = [first, second]
    for step in range(1, (size - 1) // 2 + 1):
        slots[size - step] = [shift(chunk_for(step), axis, step)]
        slots[step] = [shift(chunk_for(size - step), axis, -step)]
    slots[0] = [chunk_for(0)]
    return slots


def flat(slots):
    return jnp.concatenate([piece for slot in slots for piece in slot], 0)


def rotate(x, rows):
    return lax.dynamic_slice_in_dim(jnp.concatenate([x, x], 0), rows, x.shape[0], 0)


def per_device(
    vit_tiles,
    tile_counts,
    block_of_piece,
    segment_ids,
    text_rows,
    cotangent,
    proj_weight,
    proj_bias,
    out_weight,
    out_bias,
    ln_gain,
    ln_bias,
    norm_gain,
    v_weight,
):
    locals_ = lax.axis_size("local")
    nodes = lax.axis_size("node")
    own = lax.axis_index("local")
    node = lax.axis_index("node")
    cores = 2 if nodes % 2 == 0 else 1
    chips = nodes // cores
    core, chip = node % cores, node // cores
    order = [q ^ (q >> 1) for q in range(chips)]
    if sorted(order) != list(range(chips)):
        order = list(range(chips))
    place = [order.index(c) for c in range(chips)]
    order_table, place_table = jnp.asarray(order, jnp.int32), jnp.asarray(place, jnp.int32)
    position = place_table[chip]
    chip_ring = Ring("node", order, cores)
    local_ring = Ring("local", list(range(locals_)), 1)

    def chip_at(r):
        return order_table[(position + r) % chips]

    def swap(x):
        return lax.ppermute(x, "node", [(j, j ^ 1) for j in range(nodes)])

    blocks, share_rows, width = text_rows.shape[1:]
    kv = cotangent.shape[3]
    half_rows, features = vit_tiles.shape[2:]
    out_cols = out_weight.shape[1]
    pieces = locals_ // 2
    run_rows = share_rows // 2

    columns = proj_weight.T
    block_cols = columns.shape[0]
    weight_slots = ring_gather(columns, chip_ring)

    rows = f32(vit_tiles[0, 0])
    average = jnp.mean(rows, -1, keepdims=True)
    spread = jnp.mean((rows - average) * (rows - average), -1, keepdims=True)
    scale = lax.rsqrt(spread + 1e-05)
    slice_width = features // locals_

    def feature_slice(r):
        start = ((own + r) % locals_) * slice_width
        part = f32(lax.dynamic_slice_in_dim(vit_tiles[0, 0], start, slice_width, 1))
        gain = lax.dynamic_slice_in_dim(ln_gain, start, slice_width, 0)
        bias = lax.dynamic_slice_in_dim(ln_bias, start, slice_width, 0)
        return bf16((part - average) * scale * gain + bias)

    received = flat(exchange(feature_slice, locals_, "local"))

    doc_ids = segment_ids[0].reshape(-1)
    doc_hits = f32(doc_ids[:, None] == lax.iota(jnp.int32, DOCS)[None, :])
    own_sizes = jnp.sum(doc_hits, 0)
    doc_sizes = own_sizes
    for step in range(1, locals_):
        doc_sizes = doc_sizes + shift(own_sizes, "local", step)
    doc_weight = blocks * share_rows * locals_ / (DOCS * doc_sizes)
    token_weight = jnp.dot(doc_hits, doc_weight, precision=lax.Precision.HIGHEST)
    value_grad = bf16(f32(cotangent[0].reshape(-1, kv)) * token_weight[:, None])
    bias_part = jnp.sum(f32(value_grad), 0)

    piece_ids = lax.iota(jnp.int32, pieces)
    filled = piece_ids % SLOTS < jnp.repeat(tile_counts[0], SLOTS)
    chosen = (block_of_piece[0][None, :] == lax.iota(jnp.int32, blocks)[:, None]) & filled[None, :]
    is_text = jnp.repeat(~jnp.any(chosen, 1), share_rows)[:, None]

    shares = v_weight.shape[0]
    per_node = rotate(flat(ring_gather(v_weight, local_ring)), ((-own) % locals_) * shares)
    v_all = jnp.zeros((width, kv), v_weight.dtype)
    for r, slot in enumerate(ring_gather(per_node, chip_ring)):
        got = jnp.concatenate(slot, 0)
        start = (chip_at(r) * cores + core) * per_node.shape[0]
        v_all = lax.dynamic_update_slice_in_dim(v_all, got, start, 0)
        if cores == 2:
            start = (chip_at(r) * cores + 1 - core) * per_node.shape[0]
            v_all = lax.dynamic_update_slice_in_dim(v_all, swap(got), start, 0)

    text = f32(text_rows[0].reshape(-1, width))
    inv_text = lax.rsqrt(jnp.mean(text * text, -1, keepdims=True) + 1e-06)
    normed_text = bf16(text * inv_text * norm_gain)
    weight_text = bf16(
        lax.dot_general(
            normed_text,
            jnp.where(is_text, value_grad, jnp.zeros_like(value_grad)),
            (((0,), (0,)), ((), ())),
            preferred_element_type=jnp.float32,
        )
    )
    weight_slots_text = [
        lax.dynamic_slice_in_dim(weight_text, ((own + r) % locals_) * out_cols, out_cols, 0)
        for r in range(locals_)
    ]
    weight_sum = ring_scatter(weight_slots_text, local_ring)
    grad_text = lax.dot_general(
        value_grad, v_all, (((1,), (1,)), ((), ())), preferred_element_type=jnp.float32
    )
    gain_text = jnp.sum(jnp.where(is_text, grad_text * text * inv_text, 0.0), 0)
    scaled = grad_text * norm_gain
    hidden_grad = bf16(
        inv_text * scaled
        - text * (inv_text * inv_text * inv_text) * jnp.mean(scaled * text, -1, keepdims=True)
    ).reshape(blocks, share_rows, width)
    small = jnp.concatenate(
        [gain_text.reshape(locals_, -1), bias_part.reshape(locals_, -1)], 1
    )
    small_sum = small[own]
    for step in range(1, locals_):
        small_sum = small_sum + shift(small[(own + step) % locals_], "local", step)

    value_blocks = value_grad.reshape(blocks, share_rows, kv)
    image_values = jnp.concatenate(
        [
            jnp.where(filled[p], value_blocks[block_of_piece[0, p]], jnp.zeros((), jnp.bfloat16))
            for p in range(pieces)
        ],
        0,
    )
    image_values = rotate(
        flat(ring_gather(image_values, local_ring)), ((-own) % locals_) * image_values.shape[0]
    )
    image_values = (
        image_values.reshape(locals_, locals_, run_rows, kv).transpose(1, 0, 2, 3).reshape(-1, kv)
    )
    v_cols = lax.dynamic_slice_in_dim(v_all, own * out_cols, out_cols, 0)
    gain_cols = lax.dynamic_slice_in_dim(norm_gain, own * out_cols, out_cols, 0)
    bias_cols = lax.dynamic_slice_in_dim(out_bias, own * out_cols, out_cols, 0)
    grad_image = lax.dot_general(
        image_values, v_cols, (((1,), (1,)), ((), ())), preferred_element_type=jnp.float32
    )

    def first(part):
        return bf16(
            lax.dot_general(
                received, part, (((1,), (1,)), ((), ())), preferred_element_type=jnp.float32
            )
        )

    middle_cols = cores * block_cols
    total = None
    ranks = [0] + [r for s in range(1, (chips - 1) // 2 + 1) for r in (s, chips - s)]
    ranks += [r for r in range(chips) if r not in ranks]
    for r in ranks:
        mine = [first(part) for part in weight_slots[r]]
        if cores == 2:
            other = [first(swap(part)) for part in weight_slots[r]]
            terms = jnp.where(
                core == 0, jnp.concatenate(mine + other, 1), jnp.concatenate(other + mine, 1)
            )
        else:
            terms = jnp.concatenate(mine, 1)
        terms = lax.optimization_barrier(terms.reshape(locals_, half_rows, middle_cols))
        summed = ring_scatter([terms[s] for s in range(locals_)], local_ring)
        start = chip_at(r) * middle_cols
        bias = lax.dynamic_slice_in_dim(proj_bias, start, middle_cols, 0)
        middle = bf16(jax.nn.gelu(summed + bias, approximate=False))
        gathered = flat(ring_gather(middle, local_ring))
        second = lax.dynamic_slice_in_dim(out_weight, start, middle_cols, 0)
        product = jnp.dot(gathered, second, preferred_element_type=jnp.float32)
        total = product if total is None else total + product
    projected = bf16(total + bias_cols)
    projected = f32(rotate(projected, ((-own) % locals_) * half_rows))

    scaled_image = grad_image * gain_cols
    sums = jnp.stack([jnp.sum(projected * projected, -1), jnp.sum(scaled_image * projected, -1)])
    own_sums = sums
    for step in range(1, locals_):
        sums = sums + shift(own_sums, "local", step)
    means = sums / width
    inv_image = lax.rsqrt(means[0] + 1e-06)[:, None]
    image_grad = bf16(
        inv_image * scaled_image
        - projected * (inv_image * inv_image * inv_image) * means[1][:, None]
    ).reshape(locals_, locals_, run_rows, out_cols)
    normed_image = bf16(projected * inv_image * gain_cols)
    weight_image = lax.dot_general(
        normed_image, image_values, (((0,), (0,)), ((), ())), preferred_element_type=jnp.float32
    )
    gain_image = jnp.sum(grad_image * projected * inv_image, 0)

    slots = exchange(
        lambda r: lax.dynamic_index_in_dim(image_grad, (own + r) % locals_, 1, keepdims=False),
        locals_,
        "local",
    )
    arrived = jnp.zeros((locals_ * run_rows, width), jnp.bfloat16)
    for r, slot in enumerate(slots):
        got = jnp.concatenate(slot, 0).reshape(-1, out_cols)
        arrived = lax.dynamic_update_slice_in_dim(
            arrived, got, ((own + r) % locals_) * out_cols, 1
        )
    arrived = arrived.reshape(pieces, share_rows, width)
    for p in range(pieces):
        block = block_of_piece[0, p]
        kept = lax.dynamic_index_in_dim(hidden_grad, block, 0, keepdims=False)
        hidden_grad = lax.dynamic_update_index_in_dim(
            hidden_grad, jnp.where(filled[p], arrived[p], kept), block, 0
        )

    weight_parts = bf16(weight_sum + weight_image).reshape(chips, cores, shares, kv)
    kept = lax.dynamic_index_in_dim(weight_parts, core, 1, keepdims=False)
    if cores == 2:
        sent = lax.dynamic_index_in_dim(weight_parts, 1 - core, 1, keepdims=False)
        kept = bf16(f32(kept) + f32(swap(sent)))
    weight_own = ring_scatter([kept[chip_at(r)] for r in range(chips)], chip_ring)
    owners = [
        (n * locals_ + k, nodes * k + n) for n in range(nodes) for k in range(locals_)
    ]
    grad_weight = lax.ppermute(weight_own / nodes, ("node", "local"), owners)

    gain_sum = small_sum[:out_cols] + gain_image
    parts = jnp.concatenate(
        [gain_sum.reshape(nodes, -1), small_sum[out_cols:].reshape(nodes, -1)], 1
    )
    part_sum = parts[node]
    for step in range(1, nodes):
        part_sum = part_sum + shift(parts[(node + step) % nodes], "node", step)
    everyone = lax.all_gather(part_sum / nodes, ("local", "node"), axis=0, tiled=False)
    everyone = everyone.reshape(locals_ * nodes, -1)
    grad_gain = everyone[:, :shares].reshape(-1)
    grad_bias = everyone[:, shares:].reshape(-1)
    return (hidden_grad[None], grad_weight, grad_bias, grad_gain)


def solution(mesh):
    in_specs = (
        P("node", "local", None, None),
        P("node", None),
        P("node", None),
        P("node", None, "local"),
        P("node", None, "local", None),
        P("node", None, "local", None),
        P("local", "node"),
        P(),
        P(None, "local"),
        P(),
        P(),
        P(),
        P(),
        P(("node", "local"), None),
    )
    out_specs = (P("node", None, "local", None), P(("node", "local"), None), P(), P())
    return jax.shard_map(
        per_device, mesh=mesh, in_specs=in_specs, out_specs=out_specs, check_vma=False
    )
```

```python
import jax
import jax.numpy as jnp
from jax import lax
from jax.sharding import PartitionSpec as P

SLOTS = 2
DOCS = 16


class Ring:
    def __init__(self, axis, order, lanes):
        self.axis, self.size = axis, len(order)
        steps = range(self.size)
        self.forward = [
            (order[q] * lanes + c, order[(q + 1) % self.size] * lanes + c)
            for q in steps
            for c in range(lanes)
        ]
        self.backward = [(b, a) for a, b in self.forward]

    def up(self, x):
        return lax.ppermute(x, self.axis, self.forward)

    def down(self, x):
        return lax.ppermute(x, self.axis, self.backward)


def f32(x):
    return x.astype(jnp.float32)


def bf16(x):
    return x.astype(jnp.bfloat16)


def shift(x, axis, step):
    size = lax.axis_size(axis)
    return lax.ppermute(x, axis, [(j, (j + step) % size) for j in range(size)])


def ring_gather(x, ring):
    size = ring.size
    slots = [None] * size
    slots[0] = [x]
    ahead, behind = x, x
    for step in range(1, (size - 1) // 2 + 1):
        ahead, behind = ring.up(ahead), ring.down(behind)
        slots[size - step] = [ahead]
        slots[step] = [behind]
    if size > 1 and size % 2 == 0:
        half = x.shape[0] // 2
        slots[size // 2] = [ring.up(ahead[:half]), ring.down(behind[half:])]
    return slots


def ring_scatter(slots, ring):
    size = ring.size
    if size == 1:
        return f32(slots[0])
    half = slots[0].shape[0] // 2
    up = down = None
    if size % 2 == 0:
        up = ring.up(slots[size // 2][:half])
        down = ring.down(slots[size // 2][half:])
    partial = up is not None
    for step in range((size - 1) // 2, 0, -1):
        to_up, to_down = slots[step], slots[size - step]
        if partial:
            to_up = jnp.concatenate([bf16(f32(to_up[:half]) + f32(up)), to_up[half:]], 0)
            to_down = jnp.concatenate([to_down[:half], bf16(f32(to_down[half:]) + f32(down))], 0)
        elif up is not None:
            to_up = bf16(f32(to_up) + f32(up))
            to_down = bf16(f32(to_down) + f32(down))
        partial = False
        up, down = ring.up(to_up), ring.down(to_down)
    if partial:
        return f32(slots[0]) + jnp.concatenate([f32(up), f32(down)], 0)
    return f32(slots[0]) + f32(up) + f32(down)


def exchange(chunk_for, size, axis):
    slots = [None] * size
    middle = size // 2 if size > 1 and size % 2 == 0 else None
    if middle is not None:
        chunk = chunk_for(middle)
        half = chunk.shape[0] // 2
        first, second = shift(chunk[:half], axis, 1), shift(chunk[half:], axis, -1)
        if middle > 1:
            first, second = shift(first, axis, middle - 1), shift(second, axis, 1 - middle)
        slots[middle] = [first, second]
    for step in range(1, (size - 1) // 2 + 1):
        slots[size - step] = [shift(chunk_for(step), axis, step)]
        slots[step] = [shift(chunk_for(size - step), axis, -step)]
    slots[0] = [chunk_for(0)]
    return slots


def flat(slots):
    return jnp.concatenate([piece for slot in slots for piece in slot], 0)


def rotate(x, rows):
    return lax.dynamic_slice_in_dim(jnp.concatenate([x, x], 0), rows, x.shape[0], 0)


def per_device(
    vit_tiles,
    tile_counts,
    block_of_piece,
    segment_ids,
    text_rows,
    cotangent,
    proj_weight,
    proj_bias,
    out_weight,
    out_bias,
    ln_gain,
    ln_bias,
    norm_gain,
    v_weight,
):
    locals_ = lax.axis_size("local")
    nodes = lax.axis_size("node")
    own = lax.axis_index("local")
    node = lax.axis_index("node")
    cores = 2 if nodes % 2 == 0 else 1
    chips = nodes // cores
    core, chip = node % cores, node // cores
    order = [q ^ (q >> 1) for q in range(chips)]
    if sorted(order) != list(range(chips)):
        order = list(range(chips))
    place = [order.index(c) for c in range(chips)]
    order_table, place_table = jnp.asarray(order, jnp.int32), jnp.asarray(place, jnp.int32)
    position = place_table[chip]
    chip_ring = Ring("node", order, cores)
    local_ring = Ring("local", list(range(locals_)), 1)

    def chip_at(r):
        return order_table[(position + r) % chips]

    def swap(x):
        return lax.ppermute(x, "node", [(j, j ^ 1) for j in range(nodes)])

    blocks, share_rows, width = text_rows.shape[1:]
    kv = cotangent.shape[3]
    half_rows, features = vit_tiles.shape[2:]
    out_cols = out_weight.shape[1]
    pieces = locals_ // 2
    run_rows = share_rows // 2

    columns = proj_weight.T
    block_cols = columns.shape[0]
    weight_slots = ring_gather(columns, chip_ring)

    rows = f32(vit_tiles[0, 0])
    average = jnp.mean(rows, -1, keepdims=True)
    spread = jnp.mean((rows - average) * (rows - average), -1, keepdims=True)
    scale = lax.rsqrt(spread + 1e-05)
    slice_width = features // locals_

    def feature_slice(r):
        start = ((own + r) % locals_) * slice_width
        part = f32(lax.dynamic_slice_in_dim(vit_tiles[0, 0], start, slice_width, 1))
        gain = lax.dynamic_slice_in_dim(ln_gain, start, slice_width, 0)
        bias = lax.dynamic_slice_in_dim(ln_bias, start, slice_width, 0)
        return bf16((part - average) * scale * gain + bias)

    received = flat(exchange(feature_slice, locals_, "local"))

    doc_ids, _ = lax.optimization_barrier((segment_ids[0].reshape(-1), scale))
    doc_hits = f32(doc_ids[:, None] == lax.iota(jnp.int32, DOCS)[None, :])
    own_sizes = jnp.sum(doc_hits, 0)
    doc_sizes = own_sizes
    for step in range(1, locals_):
        doc_sizes = doc_sizes + shift(own_sizes, "local", step)
    doc_weight = blocks * share_rows * locals_ / (DOCS * doc_sizes)
    token_weight = jnp.dot(doc_hits, doc_weight, precision=lax.Precision.HIGHEST)
    value_grad = bf16(f32(cotangent[0].reshape(-1, kv)) * token_weight[:, None])
    bias_part = jnp.sum(f32(value_grad), 0)

    piece_ids = lax.iota(jnp.int32, pieces)
    filled = piece_ids % SLOTS < jnp.repeat(tile_counts[0], SLOTS)
    chosen = (block_of_piece[0][None, :] == lax.iota(jnp.int32, blocks)[:, None]) & filled[None, :]
    is_text = jnp.repeat(~jnp.any(chosen, 1), share_rows)[:, None]

    def first(part):
        return bf16(
            lax.dot_general(
                received, part, (((1,), (1,)), ((), ())), preferred_element_type=jnp.float32
            )
        )

    middle_cols = cores * block_cols

    def terms_of(r):
        mine = [first(part) for part in weight_slots[r]]
        if cores == 1:
            return jnp.concatenate(mine, 1)
        other = [first(swap(part)) for part in weight_slots[r]]
        return jnp.where(
            core == 0, jnp.concatenate(mine + other, 1), jnp.concatenate(other + mine, 1)
        )

    full = [r for s in range(1, (chips - 1) // 2 + 1) for r in (s, chips - s)]
    full_terms = [terms_of(r) for r in full]

    shares = v_weight.shape[0]
    per_node = rotate(flat(ring_gather(v_weight, local_ring)), ((-own) % locals_) * shares)
    per_node, weight_slots[chips // 2], full_terms = lax.optimization_barrier(
        (per_node, weight_slots[chips // 2], full_terms)
    )
    v_all = jnp.zeros((width, kv), v_weight.dtype)
    for r, slot in enumerate(ring_gather(per_node, chip_ring)):
        got = jnp.concatenate(slot, 0)
        start = (chip_at(r) * cores + core) * per_node.shape[0]
        v_all = lax.dynamic_update_slice_in_dim(v_all, got, start, 0)
        if cores == 2:
            start = (chip_at(r) * cores + 1 - core) * per_node.shape[0]
            v_all = lax.dynamic_update_slice_in_dim(v_all, swap(got), start, 0)

    text = f32(text_rows[0].reshape(-1, width))
    inv_text = lax.rsqrt(jnp.mean(text * text, -1, keepdims=True) + 1e-06)
    normed_text = bf16(text * inv_text * norm_gain)
    weight_text = bf16(
        lax.dot_general(
            normed_text,
            jnp.where(is_text, value_grad, jnp.zeros_like(value_grad)),
            (((0,), (0,)), ((), ())),
            preferred_element_type=jnp.float32,
        )
    )
    weight_slots_text = [
        lax.dynamic_slice_in_dim(weight_text, ((own + r) % locals_) * out_cols, out_cols, 0)
        for r in range(locals_)
    ]
    weight_sum = ring_scatter(weight_slots_text, local_ring)
    grad_text = lax.dot_general(
        value_grad, v_all, (((1,), (1,)), ((), ())), preferred_element_type=jnp.float32
    )
    gain_text = jnp.sum(jnp.where(is_text, grad_text * text * inv_text, 0.0), 0)
    scaled = grad_text * norm_gain
    hidden_grad = bf16(
        inv_text * scaled
        - text * (inv_text * inv_text * inv_text) * jnp.mean(scaled * text, -1, keepdims=True)
    ).reshape(blocks, share_rows, width)
    small = jnp.concatenate(
        [gain_text.reshape(locals_, -1), bias_part.reshape(locals_, -1)], 1
    )
    small_sum = small[own]
    for step in range(1, locals_):
        small_sum = small_sum + shift(small[(own + step) % locals_], "local", step)

    value_blocks = value_grad.reshape(blocks, share_rows, kv)
    image_values = jnp.concatenate(
        [
            jnp.where(filled[p], value_blocks[block_of_piece[0, p]], jnp.zeros((), jnp.bfloat16))
            for p in range(pieces)
        ],
        0,
    )
    image_values = rotate(
        flat(ring_gather(image_values, local_ring)), ((-own) % locals_) * image_values.shape[0]
    )
    image_values = (
        image_values.reshape(locals_, locals_, run_rows, kv).transpose(1, 0, 2, 3).reshape(-1, kv)
    )
    v_cols = lax.dynamic_slice_in_dim(v_all, own * out_cols, out_cols, 0)
    gain_cols = lax.dynamic_slice_in_dim(norm_gain, own * out_cols, out_cols, 0)
    bias_cols = lax.dynamic_slice_in_dim(out_bias, own * out_cols, out_cols, 0)
    grad_image = lax.dot_general(
        image_values, v_cols, (((1,), (1,)), ((), ())), preferred_element_type=jnp.float32
    )

    total = None
    for stage in ([0], full, [r for r in range(1, chips) if r not in full]):
        if not stage:
            continue
        starts = [chip_at(r) * middle_cols for r in stage]
        terms = full_terms if stage is full else [terms_of(r) for r in stage]
        terms = jnp.concatenate(terms, 1)
        terms = lax.optimization_barrier(terms.reshape(locals_, half_rows, -1))
        summed = ring_scatter([terms[s] for s in range(locals_)], local_ring)
        bias = jnp.concatenate(
            [lax.dynamic_slice_in_dim(proj_bias, start, middle_cols, 0) for start in starts]
        )
        middle = bf16(jax.nn.gelu(summed + bias, approximate=False))
        gathered = flat(ring_gather(middle, local_ring))
        for q, start in enumerate(starts):
            second = lax.dynamic_slice_in_dim(out_weight, start, middle_cols, 0)
            product = jnp.dot(
                gathered[:, q * middle_cols : (q + 1) * middle_cols],
                second,
                preferred_element_type=jnp.float32,
            )
            total = product if total is None else total + product
    projected = bf16(total + bias_cols)
    projected = f32(rotate(projected, ((-own) % locals_) * half_rows))

    scaled_image = grad_image * gain_cols
    sums = jnp.stack([jnp.sum(projected * projected, -1), jnp.sum(scaled_image * projected, -1)])
    own_sums = sums
    for step in range(1, locals_):
        sums = sums + shift(own_sums, "local", step)
    means = sums / width
    inv_image = lax.rsqrt(means[0] + 1e-06)[:, None]
    image_grad = bf16(
        inv_image * scaled_image
        - projected * (inv_image * inv_image * inv_image) * means[1][:, None]
    ).reshape(locals_, locals_, run_rows, out_cols)
    normed_image = bf16(projected * inv_image * gain_cols)
    weight_image = lax.dot_general(
        normed_image, image_values, (((0,), (0,)), ((), ())), preferred_element_type=jnp.float32
    )
    gain_image = jnp.sum(grad_image * projected * inv_image, 0)

    slots = exchange(
        lambda r: lax.dynamic_index_in_dim(image_grad, (own + r) % locals_, 1, keepdims=False),
        locals_,
        "local",
    )
    arrived = jnp.zeros((locals_ * run_rows, width), jnp.bfloat16)
    for r, slot in enumerate(slots):
        got = jnp.concatenate(slot, 0).reshape(-1, out_cols)
        arrived = lax.dynamic_update_slice_in_dim(
            arrived, got, ((own + r) % locals_) * out_cols, 1
        )
    arrived = arrived.reshape(pieces, share_rows, width)
    for p in range(pieces):
        block = block_of_piece[0, p]
        kept = lax.dynamic_index_in_dim(hidden_grad, block, 0, keepdims=False)
        hidden_grad = lax.dynamic_update_index_in_dim(
            hidden_grad, jnp.where(filled[p], arrived[p], kept), block, 0
        )

    gain_sum = small_sum[:out_cols] + gain_image
    extra = jnp.concatenate(
        [gain_sum.reshape(nodes, -1), small_sum[out_cols:].reshape(nodes, -1)], 1
    )
    extra_size = extra.shape[1]
    extra_rows = -(-extra_size // (16 * kv)) * 16
    extra = jnp.pad(extra, ((0, 0), (0, extra_rows * kv - extra_size)))
    weight_parts = bf16(
        jnp.concatenate(
            [
                (weight_sum + weight_image).reshape(nodes, shares, kv),
                extra.reshape(nodes, extra_rows, kv),
            ],
            1,
        )
    ).reshape(chips, cores, shares + extra_rows, kv)
    kept = lax.dynamic_index_in_dim(weight_parts, core, 1, keepdims=False)
    if cores == 2:
        sent = lax.dynamic_index_in_dim(weight_parts, 1 - core, 1, keepdims=False)
        kept = bf16(f32(kept) + f32(swap(sent)))
    own_parts = ring_scatter([kept[chip_at(r)] for r in range(chips)], chip_ring) / nodes
    owners = [
        (n * locals_ + k, nodes * k + n) for n in range(nodes) for k in range(locals_)
    ]
    grad_weight = lax.ppermute(own_parts[:shares], ("node", "local"), owners)

    everyone = own_parts[shares:].reshape(1, -1)[:, :extra_size]
    for axis, size, index in (("local", locals_, own), ("node", nodes, node)):
        copies = [everyone] + [shift(everyone, axis, -step) for step in range(1, size)]
        copies = jnp.stack(copies + copies, 0)
        everyone = lax.dynamic_slice_in_dim(copies, (-index) % size, size, 0)
    everyone = everyone.reshape(nodes, locals_, extra_size).transpose(1, 0, 2)
    grad_gain = everyone[:, :, :shares].reshape(-1)
    grad_bias = everyone[:, :, shares:].reshape(-1)
    return (hidden_grad[None], grad_weight, grad_bias, grad_gain)


def solution(mesh):
    in_specs = (
        P("node", "local", None, None),
        P("node", None),
        P("node", None),
        P("node", None, "local"),
        P("node", None, "local", None),
        P("node", None, "local", None),
        P("local", "node"),
        P(),
        P(None, "local"),
        P(),
        P(),
        P(),
        P(),
        P(("node", "local"), None),
    )
    out_specs = (P("node", None, "local", None), P(("node", "local"), None), P(), P())
    return jax.shard_map(
        per_device, mesh=mesh, in_specs=in_specs, out_specs=out_specs, check_vma=False
    )
```
